128 devices in a mesh: seq: 32 (over y, x, core), chan: 4 (over z).
Axes of the slice: x: 4, y: 4, z: 4, core: 2. Of those that a mesh axis runs over, the one named last changes fastest.
Arguments:
- query_in: bfloat16 [16384, 4096], P('seq', 'chan'), may hold values from -6 to 6
- key_in: bfloat16 [16384, 4096], P('seq', 'chan'), may hold values from -6 to 6
- value_in: bfloat16 [16384, 4096], P('seq', 'chan'), may hold values from -6 to 6
- decay_time: float32 [4096, 16], P('chan'), may hold values from 30 to 65536
- residue: float32 [4096, 16], P('chan'), may hold values from -27 to 27
- out_weight: bfloat16 [4096, 4096], P('chan'), may hold values from -0.09375 to 0.09375
- cotangent: bfloat16 [16384, 4096], P('seq', 'chan'), may hold values from -6 to 6
Outputs:
- mixed_out: bfloat16 [16384, 4096], P('seq', 'chan')
- query_grad: bfloat16 [16384, 4096], P('seq', 'chan')
- key_grad: bfloat16 [16384, 4096], P('seq', 'chan')
- value_grad: bfloat16 [16384, 4096], P('seq', 'chan')
- residue_grad: float32 [4096, 16], P('chan')
The draws below stay inside these ranges and needn't reach their ends.
All inputs are finite; a program needn't handle non-finite values.
Results may differ from the reference program's by a relative error of at most 0.02.
Values may be sent and summed in bfloat16 or wider, within the bound.
No kernel may reach another device: no remote copies, remote signals or barrier semaphores. Data moves between devices by JAX's collectives and lax.ppermute only.
A program may use at most 192 MiB of HBM per device.

```python
import math
import jax
import jax.numpy as jnp
from jax import lax

CHANNELS = 4096
MODES = 16
TOKENS = 16384
N_CHAN = 4


def modal_groups(key, slow_share):
    base_key = jax.random.fold_in(key, 7001)
    kind_key, slow_key, quick_key, size_key, sign_key, mix_key, free_key = jax.random.split(base_key, 7)
    group_count = MODES // 4
    spacing = 0.5
    group_span = 3.0 * spacing
    is_slow = jax.random.uniform(kind_key, (CHANNELS, group_count), jnp.float32) < slow_share
    slow_fastest = jnp.exp(jax.random.uniform(slow_key, (CHANNELS, group_count), jnp.float32, math.log(TOKENS / 8.0), math.log(4.0 * TOKENS) - group_span))
    quick_fastest = jnp.exp(jax.random.uniform(quick_key, (CHANNELS, group_count), jnp.float32, math.log(30.0), math.log(max(40.0, TOKENS / 36.0))))
    fastest = jnp.where(is_slow, slow_fastest, quick_fastest)
    offsets = spacing * (3.0 - jnp.arange(4, dtype=jnp.float32))
    time_table = fastest[:, :, None] * jnp.exp(offsets)[None, None, :]
    decay_time = jnp.clip(time_table.reshape(CHANNELS, MODES), 30.0, 4.0 * TOKENS)
    amplitude = jnp.exp(jax.random.uniform(size_key, (CHANNELS, group_count), jnp.float32, 0.0, math.log(3.0)))
    amplitude = amplitude * jnp.where(is_slow, 3.0, 1.5)
    sign_flip = jnp.where(jax.random.uniform(sign_key, (CHANNELS, group_count), jnp.float32) < 0.5, -1.0, 1.0)
    pattern = jnp.array([1.0, -3.0, 3.0, -1.0], jnp.float32)
    structured = (sign_flip * amplitude)[:, :, None] * pattern[None, None, :]
    free_part = jnp.clip(0.25 * jax.random.normal(free_key, (CHANNELS, group_count, 4), jnp.float32), -1.5, 1.5)
    is_free = jax.random.uniform(mix_key, (CHANNELS, group_count), jnp.float32) < 0.25
    residue = jnp.where(is_free[:, :, None], free_part, structured).reshape(CHANNELS, MODES)
    residue = jnp.clip(residue, -27.0, 27.0)
    return (decay_time.astype(jnp.float32), residue.astype(jnp.float32))


def draw_decay_time(key, part):
    slow_share = 0.5
    return modal_groups(key, slow_share)[0]


def draw_residue(key, part):
    slow_share = 0.5
    return modal_groups(key, slow_share)[1]


def block_levels(key, shape, pieces, smallest, top_value):
    def one(position, parts):
        steps = jax.random.uniform(jax.random.fold_in(jax.random.fold_in(key, 6), position), (parts,), jnp.float32, smallest / len(pieces), top_value / len(pieces))
        return jnp.repeat(jnp.exp(steps), shape[position] // parts).reshape((-1,) + (1,) * (len(shape) - position - 1))

    gain = one(*pieces[0])
    for cut in pieces[1:]:
        gain = gain * one(*cut)
    return gain


def normal_values(own_key, shape, width, bound, pieces=(), kind=jnp.bfloat16):
    drawn = width * jax.random.normal(own_key, shape, jnp.float32)
    if pieces:
        drawn = drawn * block_levels(own_key, shape, pieces, -0.22, 0.18)
    return jnp.clip(drawn, -bound, bound).astype(kind)


def setup_inputs(seed: int = 0) -> dict:
    keys = jax.random.split(jax.random.key(seed), 8)
    query_in = normal_values(keys[0], (TOKENS, CHANNELS), 1.0, 6.0, ((0, 32), (1, 4)))
    key_in = normal_values(keys[1], (TOKENS, CHANNELS), 1.0, 6.0, ((0, 32), (1, 4)))
    value_in = normal_values(keys[2], (TOKENS, CHANNELS), 1.0, 6.0, ((0, 32), (1, 4)))
    decay_time = draw_decay_time(jax.random.fold_in(keys[7], 71), 0)
    residue = draw_residue(jax.random.fold_in(keys[7], 71), 0)
    out_weight = normal_values(keys[5], (CHANNELS, CHANNELS), CHANNELS ** -0.5, 0.09375, ((0, 4),))
    cotangent = normal_values(keys[6], (TOKENS, CHANNELS), 1.0, 6.0, ((0, 32), (1, 4)))
    return dict(query_in=query_in, key_in=key_in, value_in=value_in, decay_time=decay_time, residue=residue, out_weight=out_weight, cotangent=cotangent)


def reference(query_in, key_in, value_in, decay_time, residue, out_weight, cotangent):
    decay_rate = 1.0 / decay_time
    decay_step = jnp.exp(-decay_rate)
    norm_factor = jnp.sqrt(-jnp.expm1(-2.0 * decay_rate))
    mode_gain = norm_factor * residue
    product = (key_in.astype(jnp.float32) * value_in.astype(jnp.float32)).astype(jnp.bfloat16)
    grad_gated = jnp.dot(cotangent, out_weight.T, preferred_element_type=jnp.float32)
    weighted = (grad_gated * query_in.astype(jnp.float32)).astype(jnp.bfloat16)
    empty_modes = jnp.zeros(decay_step.shape, jnp.float32)

    def forward(carried, inputs):
        modal, correlation = carried
        product_row, weighted_row = inputs
        modal = decay_step * modal + product_row.astype(jnp.float32)[:, None]
        correlation = correlation + weighted_row.astype(jnp.float32)[:, None] * modal
        return ((modal, correlation), lax.optimization_barrier(jnp.sum(mode_gain * modal, axis=1)))
    (modal_end, correlation), convolved = lax.scan(forward, (empty_modes, empty_modes), (product, weighted))

    def backward(modal, weighted_row):
        modal = decay_step * modal + weighted_row.astype(jnp.float32)[:, None]
        return (modal, lax.optimization_barrier(jnp.sum(mode_gain * modal, axis=1)))
    back_end, grad_product = lax.scan(backward, empty_modes, weighted, reverse=True)
    gated = (query_in.astype(jnp.float32) * convolved).astype(jnp.bfloat16)
    group_size = CHANNELS // N_CHAN
    summed = jnp.zeros((TOKENS, CHANNELS), jnp.float32)
    for group_index in range(N_CHAN):
        first = group_index * group_size
        rounded_part = jnp.dot(gated[:, first:first + group_size], out_weight[first:first + group_size], preferred_element_type=jnp.float32).astype(jnp.bfloat16)
        summed = summed + lax.optimization_barrier(rounded_part).astype(jnp.float32)
    mixed_out = summed.astype(jnp.bfloat16)
    query_grad = (grad_gated * convolved).astype(jnp.bfloat16)
    key_grad = (grad_product * value_in.astype(jnp.float32)).astype(jnp.bfloat16)
    value_grad = (grad_product * key_in.astype(jnp.float32)).astype(jnp.bfloat16)
    residue_grad = norm_factor * correlation / jnp.sqrt(jnp.float32(TOKENS))
    return (mixed_out, query_grad, key_grad, value_grad, residue_grad)
```

```python
import jax
import jax.numpy as jnp
from jax import lax
from jax.experimental import pallas as pl
from jax.experimental.pallas import tpu as pltpu
from jax.sharding import PartitionSpec as P

LANES = 128
CHUNK = 16


def cost(steps, ops):
    return pl.CostEstimate(flops=steps * ops * 1024, transcendentals=0, bytes_accessed=1 << 22)


def spread_rows(target, rows, start, groups):
    for index in range(groups):
        target[pl.ds(start * groups + index, rows.shape[0], stride=groups), :] = rows[
            :, index * LANES : (index + 1) * LANES
        ]


def forward_states(key_ref, value_ref, decay_ref, tiles_ref, end_ref):
    row_count, width = key_ref.shape
    groups = width // LANES
    modes = decay_ref.shape[0]
    chunks = row_count // CHUNK

    def fill(index):
        start = pl.multiple_of(index * CHUNK, CHUNK)
        rows = key_ref[pl.ds(start, CHUNK), :].astype(jnp.float32) * value_ref[
            pl.ds(start, CHUNK), :
        ].astype(jnp.float32)
        spread_rows(tiles_ref, rows.astype(jnp.bfloat16).astype(jnp.float32), start, groups)

    def advance(index, states):
        base = pl.multiple_of(index * CHUNK * groups, CHUNK * groups)
        for step in range(CHUNK):
            tile = tiles_ref[pl.ds(base + step * groups, groups), :]
            states = tuple(decay_ref[n] * states[n] + tile for n in range(modes))
        return states

    def body(index, states):
        states = advance(index, states)
        fill(index + 1)
        return states

    fill(0)
    empty = tuple(jnp.zeros((groups, LANES), jnp.float32) for _ in range(modes))
    states = lax.fori_loop(0, chunks - 1, body, empty)
    states = advance(chunks - 1, states)
    for n in range(modes):
        end_ref[n] = states[n]


def forward_values(tiles_ref, decay_ref, gain_ref, carry_ref, query_ref, conv_ref, gated_ref, sums_ref):
    row_count, width = query_ref.shape
    groups = width // LANES
    modes = decay_ref.shape[0]
    chunks = row_count // CHUNK

    def advance(index, states):
        base = pl.multiple_of(index * CHUNK * groups, CHUNK * groups)
        for step in range(CHUNK):
            tile = tiles_ref[pl.ds(base + step * groups, groups), :]
            states = tuple(decay_ref[n] * states[n] + tile for n in range(modes))
            sums_ref[pl.ds(base + step * groups, groups), :] = weighted_sum(gain_ref, states)
        return states

    def emit(index):
        start = pl.multiple_of(index * CHUNK, CHUNK)
        for part in range(groups):
            conv = sums_ref[pl.ds(start * groups + part, CHUNK, stride=groups), :]
            lanes = slice(part * LANES, (part + 1) * LANES)
            conv_ref[pl.ds(start, CHUNK), lanes] = conv
            query = query_ref[pl.ds(start, CHUNK), lanes].astype(jnp.float32)
            gated_ref[pl.ds(start, CHUNK), lanes] = (query * conv).astype(jnp.bfloat16)

    def body(index, states):
        emit(index - 1)
        return advance(index, states)

    states = advance(0, tuple(carry_ref[n] for n in range(modes)))
    lax.fori_loop(1, chunks, body, states)
    emit(chunks - 1)


def weighted_sum(gain_ref, states):
    terms = [gain_ref[n] * states[n] for n in range(len(states))]
    while len(terms) > 1:
        terms = [terms[i] + terms[i + 1] for i in range(0, len(terms), 2)]
    return terms[0]


def backward_states(weighted_ref, tiles_ref, decay_ref, back_tiles_ref, start_ref, corr_ref):
    row_count, width = weighted_ref.shape
    groups = width // LANES
    modes = decay_ref.shape[0]
    chunks = row_count // CHUNK

    def fill(index):
        start = pl.multiple_of(index * CHUNK, CHUNK)
        rows = weighted_ref[pl.ds(start, CHUNK), :].astype(jnp.float32)
        spread_rows(back_tiles_ref, rows, start, groups)

    def advance(index, carried):
        states, sums = carried
        base = pl.multiple_of(index * CHUNK * groups, CHUNK * groups)
        for step in reversed(range(CHUNK)):
            back_tile = back_tiles_ref[pl.ds(base + step * groups, groups), :]
            tile = tiles_ref[pl.ds(base + step * groups, groups), :]
            states = tuple(decay_ref[n] * states[n] + back_tile for n in range(modes))
            sums = tuple(sums[n] + tile * states[n] for n in range(modes))
        return (states, sums)

    def body(step, carried):
        index = chunks - 1 - step
        carried = advance(index, carried)
        fill(index - 1)
        return carried

    fill(chunks - 1)
    empty = tuple(jnp.zeros((groups, LANES), jnp.float32) for _ in range(modes))
    carried = lax.fori_loop(0, chunks - 1, body, (empty, empty))
    states, sums = advance(0, carried)
    for n in range(modes):
        start_ref[n] = states[n]
        corr_ref[n] = sums[n]


def backward_values(
    back_tiles_ref, decay_ref, gain_ref, carry_ref, key_ref, value_ref, key_out, value_out, sums_ref
):
    row_count, width = key_ref.shape
    groups = width // LANES
    modes = decay_ref.shape[0]
    chunks = row_count // CHUNK

    def advance(index, states):
        base = pl.multiple_of(index * CHUNK * groups, CHUNK * groups)
        for step in reversed(range(CHUNK)):
            tile = back_tiles_ref[pl.ds(base + step * groups, groups), :]
            states = tuple(decay_ref[n] * states[n] + tile for n in range(modes))
            sums_ref[pl.ds(base + step * groups, groups), :] = weighted_sum(gain_ref, states)
        return states

    def emit(index):
        start = pl.multiple_of(index * CHUNK, CHUNK)
        for part in range(groups):
            grad = sums_ref[pl.ds(start * groups + part, CHUNK, stride=groups), :]
            lanes = slice(part * LANES, (part + 1) * LANES)
            value = value_ref[pl.ds(start, CHUNK), lanes].astype(jnp.float32)
            key = key_ref[pl.ds(start, CHUNK), lanes].astype(jnp.float32)
            key_out[pl.ds(start, CHUNK), lanes] = (grad * value).astype(jnp.bfloat16)
            value_out[pl.ds(start, CHUNK), lanes] = (grad * key).astype(jnp.bfloat16)

    def body(step, states):
        index = chunks - 1 - step
        emit(index + 1)
        return advance(index, states)

    states = advance(chunks - 1, tuple(carry_ref[n] for n in range(modes)))
    lax.fori_loop(1, chunks, body, states)
    emit(0)


def forward_carries(ends_ref, span_ref, carries_ref):
    carry = jnp.zeros(span_ref.shape, jnp.float32)
    for place in range(ends_ref.shape[0]):
        carries_ref[place] = carry
        carry = span_ref[...] * carry + ends_ref[place]


def backward_carries(both_ref, ends_ref, span_ref, decay_ref, scale_ref, out_ref):
    places, rows, _ = ends_ref.shape
    carry = jnp.zeros(span_ref.shape, jnp.float32)
    total = jnp.zeros(span_ref.shape, jnp.float32)
    crossed = jnp.zeros(span_ref.shape, jnp.float32)
    for place in reversed(range(places)):
        out_ref[place, :rows] = carry
        crossed = crossed + ends_ref[place] * carry
        total = total + both_ref[place, rows:]
        carry = span_ref[...] * carry + both_ref[place, :rows]
    result = scale_ref[...] * (total + decay_ref[...] * crossed)
    for place in range(places):
        out_ref[place, rows:] = result


def shaped(shape, dtype):
    return jax.ShapeDtypeStruct(shape, dtype)


def swap(array):
    return lax.all_to_all(array, "seq", split_axis=0, concat_axis=0, tiled=True)


def per_device(query_in, key_in, value_in, decay_time, residue, out_weight, cotangent):
    row_count, width = query_in.shape
    modes = decay_time.shape[1]
    groups = width // LANES
    seq_count = lax.axis_size("seq")
    chan_count = lax.axis_size("chan")
    assert chan_count == 4
    seat = lax.axis_index("chan")
    up = [(i, (i + 1) % chan_count) for i in range(chan_count)]
    down = [(i, (i - 1) % chan_count) for i in range(chan_count)]
    half = width // 2

    below = lax.ppermute(cotangent, "chan", up)
    above = lax.ppermute(cotangent, "chan", down)
    across_low = lax.ppermute(below[:, :half], "chan", up)
    across_high = lax.ppermute(above[:, half:], "chan", down)

    rate = (1.0 / decay_time).T
    decay = jnp.exp(-rate)
    norm = jnp.sqrt(-jnp.expm1(-2.0 * rate))
    gain = norm * residue.T
    tile_shape = (modes, groups, LANES)
    decay_tiles = decay.reshape(tile_shape)
    gain_tiles = gain.reshape(tile_shape)
    part_rows = modes * groups // seq_count
    part_shape = (seq_count, part_rows, LANES)
    place = lax.axis_index("seq")
    own_rate = lax.dynamic_index_in_dim(rate.reshape(part_shape), place, 0, keepdims=False)
    own_decay = jnp.exp(-own_rate)
    own_span = jnp.exp(-own_rate * row_count)
    own_scale = jnp.sqrt(-jnp.expm1(-2.0 * own_rate)) / jnp.sqrt(
        jnp.float32(row_count * seq_count)
    )

    tiled = (row_count * groups, LANES)
    tiles, end_states = pl.pallas_call(
        forward_states,
        out_shape=(shaped(tiled, jnp.float32), shaped(tile_shape, jnp.float32)),
        cost_estimate=cost(row_count, 2 * modes),
        name="forward_states",
    )(key_in, value_in, decay_tiles)
    ends = swap(end_states.reshape(part_shape))
    carries = pl.pallas_call(
        forward_carries, out_shape=shaped(part_shape, jnp.float32), name="forward_carries"
    )(ends, own_span)
    carry_in = swap(carries).reshape(tile_shape)
    convolved, gated = pl.pallas_call(
        forward_values,
        out_shape=(
            shaped((row_count, width), jnp.float32),
            shaped((row_count, width), jnp.bfloat16),
        ),
        scratch_shapes=[pltpu.VMEM(tiled, jnp.float32)],
        cost_estimate=cost(row_count, 4 * modes),
        name="forward_values",
    )(tiles, decay_tiles, gain_tiles, carry_in, query_in)

    def block_of(offset):
        return ((seat + offset) % chan_count) * width

    def project(offset, size):
        columns = lax.dynamic_slice_in_dim(out_weight, offset, size, 1)
        return jnp.dot(gated, columns, preferred_element_type=jnp.float32).astype(jnp.bfloat16)

    far = project(block_of(2), width)
    far_low = lax.ppermute(far[:, :half], "chan", up)
    far_high = lax.ppermute(far[:, half:], "chan", down)
    upper = project(block_of(1), width)
    lower = project(block_of(3), width)
    upper_high = lax.ppermute(upper[:, half:], "chan", up)
    lower_low = lax.ppermute(lower[:, :half], "chan", down)
    own_out = project(block_of(0), width)

    def join(first, second):
        return (first.astype(jnp.float32) + second.astype(jnp.float32)).astype(jnp.bfloat16)

    upper_low = lax.ppermute(join(upper[:, :half], far_low), "chan", up)
    lower_high = lax.ppermute(join(lower[:, half:], far_high), "chan", down)
    from_below = jnp.concatenate([upper_low, upper_high], axis=1)
    from_above = jnp.concatenate([lower_low, lower_high], axis=1)
    mixed_out = (
        own_out.astype(jnp.float32)
        + from_below.astype(jnp.float32)
        + from_above.astype(jnp.float32)
    ).astype(jnp.bfloat16)

    def pull(block, offset):
        columns = lax.dynamic_slice_in_dim(out_weight, offset, block.shape[1], 1)
        return lax.dot_general(
            block, columns, (((1,), (1,)), ((), ())), preferred_element_type=jnp.float32
        )

    across = jnp.concatenate([across_low, across_high], axis=1)
    grad_gated = (
        pull(cotangent, block_of(0))
        + pull(below, block_of(3))
        + pull(above, block_of(1))
        + pull(across, block_of(2))
    )
    weighted = (grad_gated * query_in.astype(jnp.float32)).astype(jnp.bfloat16)
    query_grad = (grad_gated * convolved).astype(jnp.bfloat16)

    back_tiles, start_states, local_corr = pl.pallas_call(
        backward_states,
        out_shape=(
            shaped(tiled, jnp.float32),
            shaped(tile_shape, jnp.float32),
            shaped(tile_shape, jnp.float32),
        ),
        cost_estimate=cost(row_count, 4 * modes),
        name="backward_states",
    )(weighted, tiles, decay_tiles)
    both = swap(
        jnp.concatenate(
            [start_states.reshape(part_shape), local_corr.reshape(part_shape)], axis=1
        )
    )
    back_and_grad = pl.pallas_call(
        backward_carries,
        out_shape=shaped((seq_count, 2 * part_rows, LANES), jnp.float32),
        name="backward_carries",
    )(both, ends, own_span, own_decay, own_scale)
    back_and_grad = swap(back_and_grad)
    carry_back = back_and_grad[:, :part_rows].reshape(tile_shape)
    residue_grad = back_and_grad[:, part_rows:].reshape(modes, width).T
    key_grad, value_grad = pl.pallas_call(
        backward_values,
        out_shape=(
            shaped((row_count, width), jnp.bfloat16),
            shaped((row_count, width), jnp.bfloat16),
        ),
        scratch_shapes=[pltpu.VMEM(tiled, jnp.float32)],
        cost_estimate=cost(row_count, 4 * modes),
        name="backward_values",
    )(back_tiles, decay_tiles, gain_tiles, carry_back, key_in, value_in)
    return (mixed_out, query_grad, key_grad, value_grad, residue_grad)


def solution(mesh):
    in_specs = (
        P("seq", "chan"),
        P("seq", "chan"),
        P("seq", "chan"),
        P("chan", None),
        P("chan", None),
        P("chan", None),
        P("seq", "chan"),
    )
    out_specs = (
        P("seq", "chan"),
        P("seq", "chan"),
        P("seq", "chan"),
        P("seq", "chan"),
        P("chan", None),
    )
    return jax.shard_map(
        per_device, mesh=mesh, in_specs=in_specs, out_specs=out_specs, check_vma=False
    )
```
